32 devices in a mesh: groups: 2 (over x), shot: 16 (over z, y, core).
Axes of the slice: x: 2, y: 2, z: 4, core: 2. Of those that a mesh axis runs over, the one named last changes fastest.
Arguments:
- spectra: bfloat16 [1024, 2, 64, 512], P(('groups', 'shot')), parts along dimension 0, may hold values from -1.1953125 to 1.1953125
- fold_counts: int32 [1024], P('groups'), parts along dimension 0, may hold values from 1 to 512
- inverse_wavelet: float32 [2, 64], replicated, may hold values from -4 to 4
Outputs:
- multiples: bfloat16 [1024, 2, 64, 512], P(('groups', 'shot')), parts along dimension 0
The draws below stay inside these ranges and needn't reach their ends.
There are 2 independent parts, one for each index of `groups`. The reference program is written for one: setup_inputs(seed, part) draws one part's arguments, and reference() takes and returns one part's arrays. A program takes and returns all parts, laid end to end along the dimension named above; an argument that names none is the same for every part. Nothing has to cross between parts.
All inputs are finite; a program needn't handle non-finite values.
Results may differ from the reference program's by a relative error of at most 0.001.
Values may be sent and summed in bfloat16 or wider, within the bound.
A program may use at most 64 MiB of HBM per device.

```python
import jax
import jax.numpy as jnp
from jax import lax

POINTS = 512
BINS = 64


def draw_fold_counts(key, part):
    key_choose = jax.random.fold_in(key, 11)
    key_wide = jax.random.fold_in(key, 12)
    key_pick = jax.random.fold_in(key, 13)
    chooser = jax.random.randint(key_choose, (POINTS,), 0, 2)
    wide = jax.random.randint(key_wide, (POINTS,), POINTS // 2 + 1, POINTS + 1)
    folds = jnp.where(chooser == 1, wide, 1)
    picks = jax.random.permutation(key_pick, POINTS)
    positions = jnp.arange(POINTS, dtype=jnp.int32)
    folds = jnp.where(positions == picks[0], POINTS, folds)
    folds = jnp.where(positions == picks[1], 1, folds)
    return folds.astype(jnp.int32)


def levels(stream_key, dims, split, low, high):
    factor_of, own = 1.0, jax.random.fold_in(stream_key, 6)
    for axis_at, parts in split:
        draws = jnp.exp(jax.random.uniform(jax.random.fold_in(own, axis_at), (parts,), jnp.float32, low / len(split), high / len(split)))
        factor_of = factor_of * jnp.repeat(draws, dims[axis_at] // parts).reshape([-1 if axis == axis_at else 1 for axis in range(len(dims))])
    return factor_of


def bell_draw(stream_key, extent, width, reach, cuts=(), kind=jnp.bfloat16):
    array = width * jax.random.normal(stream_key, extent, jnp.float32)
    if cuts:
        array = array * levels(stream_key, extent, cuts, -0.22, 0.18)
    return jnp.clip(array, -reach, reach).astype(kind)


def setup_inputs(seed: int = 0, part: int = 0) -> dict:
    arg_keys = jax.random.split(jax.random.key(seed), 4)
    part_keys = jax.random.split(jax.random.fold_in(arg_keys[3], part), 4)
    spectra = bell_draw(part_keys[0], (POINTS, 2, BINS, POINTS), 0.2, 1.1953125, ((0, 16),))
    fold_counts = draw_fold_counts(jax.random.fold_in(jax.random.fold_in(arg_keys[3], part), 71), part)
    inverse_wavelet = bell_draw(arg_keys[2], (2, BINS), 1.0, 4.0, (), jnp.float32)
    return dict(spectra=spectra, fold_counts=fold_counts, inverse_wavelet=inverse_wavelet)


def reference(spectra, fold_counts, inverse_wavelet):
    indices = jnp.arange(POINTS, dtype=jnp.int32)
    recorded = jnp.abs(indices[None, :] - indices[:, None]) < fold_counts[:, None]
    mirrored = spectra.transpose(3, 1, 2, 0)
    filled = jnp.where(recorded[:, None, None, :], spectra,
                       jnp.where(recorded.T[:, None, None, :], mirrored, jnp.zeros_like(spectra)))

    def per_bin(which):
        slab = lax.dynamic_index_in_dim(filled, which, 2, keepdims=False)
        real_component = slab[:, 0, :]
        imaginary_component = slab[:, 1, :]
        prod_real = jnp.dot(real_component, real_component, preferred_element_type=jnp.float32) - jnp.dot(imaginary_component, imaginary_component, preferred_element_type=jnp.float32)
        prod_imag = jnp.dot(real_component, imaginary_component, preferred_element_type=jnp.float32) + jnp.dot(imaginary_component, real_component, preferred_element_type=jnp.float32)
        wave = lax.dynamic_index_in_dim(inverse_wavelet, which, 1, keepdims=False)
        output_real = -(wave[0] * prod_real - wave[1] * prod_imag)
        out_imag = -(wave[0] * prod_imag + wave[1] * prod_real)
        return jnp.stack([output_real, out_imag], axis=1).astype(jnp.bfloat16)

    stacked_spectra = lax.map(per_bin, jnp.arange(BINS, dtype=jnp.int32))
    return stacked_spectra.transpose(1, 2, 0, 3)
```

```python
import functools

import jax
import jax.numpy as jnp
from jax import lax
from jax.experimental import pallas as pl
from jax.experimental.pallas import tpu as pltpu
from jax.sharding import PartitionSpec as P

MESH = pl.DeviceIdType.MESH
VMEM_BYTES = 56 * 1024 * 1024


def exchange_kernel(n, x_ref, col_ref, row_ref, wave_ref, o_ref,
                    stage, send, recv, prod, landed, keep, swap, eye,
                    in_send, in_recv, out_send, out_recv, own_out, load_sem):
    shots, _, bins, points = x_ref.shape
    local = bins // n
    me = lax.axis_index("shot")
    mine = pl.ds(pl.multiple_of(me * shots, shots), shots)
    barrier = pltpu.get_barrier_semaphore()

    @pl.loop(1, n)
    def _(k):
        pl.semaphore_signal(barrier, inc=1, device_id={"shot": lax.rem(me + k, n)}, device_id_type=MESH)

    @pl.loop(0, shots)
    def _(s):
        rows = x_ref[s].reshape(2 * bins, points).astype(jnp.float32)
        for q in range(points // 128):
            stage[q, pl.ds(pl.multiple_of(s * 2 * bins, 2 * bins), 2 * bins), :] = rows[:, q * 128 : q * 128 + 128]

    @pl.loop(0, bins)
    def _(f):
        for c in range(2):
            for q in range(points // 128):
                lanes = pl.ds(q * 128, 128)
                send[f, c, :, lanes] = stage[q, pl.ds(c * bins + f, shots, stride=2 * bins), :].astype(jnp.bfloat16)

    pl.semaphore_wait(barrier, n - 1)

    @pl.loop(0, local)
    def _(j):
        pltpu.make_async_copy(send.at[me * local + j], recv.at[j, :, mine, :], in_recv.at[j]).start()

        @pl.loop(1, n)
        def _(k):
            to = lax.rem(me + k, n)
            pltpu.make_async_remote_copy(
                send.at[to * local + j], recv.at[j, :, mine, :], in_send, in_recv.at[j],
                device_id={"shot": to}, device_id_type=MESH).start()

    shot = lax.broadcasted_iota(jnp.int32, (points, points), 0)
    point = lax.broadcasted_iota(jnp.int32, (points, points), 1)
    apart = jnp.abs(shot - point)
    direct = apart < col_ref[...]
    mirrored = apart < row_ref[...]
    keep[...] = jnp.where(direct, 1.0, 0.0).astype(jnp.bfloat16)
    swap[...] = jnp.where(jnp.logical_and(direct, jnp.logical_not(mirrored)), 1.0, 0.0).astype(jnp.bfloat16)
    eye[...] = jnp.where(shot == point, 1.0, 0.0).astype(jnp.bfloat16)

    @pl.loop(0, local)
    def _(j):
        pltpu.make_async_copy(recv.at[j], recv.at[j], in_recv.at[j]).wait()
        for c in range(2):
            block = recv[j, c]
            turned = lax.dot_general(eye[...], block * swap[...], (((1,), (1,)), ((), ())),
                                     preferred_element_type=jnp.float32).astype(jnp.bfloat16)
            recv[j, c] = block * keep[...] + turned
        wave_real = wave_ref[0, me * local + j]
        wave_imag = wave_ref[1, me * local + j]
        tile = min(points, 256)

        @pl.loop(0, points // tile)
        def _(t):
            part = pl.ds(pl.multiple_of(t * tile, tile), tile)
            left_real, left_imag = recv[j, 0, part, :], recv[j, 1, part, :]
            real, imag = recv[j, 0], recv[j, 1]
            dot = functools.partial(jnp.dot, preferred_element_type=jnp.float32)
            prod_real = dot(left_real, real) - dot(left_imag, imag)
            prod_imag = dot(left_real, imag) + dot(left_imag, real)
            prod[j, 0, part, :] = (-(wave_real * prod_real - wave_imag * prod_imag)).astype(jnp.bfloat16)
            prod[j, 1, part, :] = (-(wave_real * prod_imag + wave_imag * prod_real)).astype(jnp.bfloat16)

        pltpu.make_async_copy(prod.at[j, :, mine, :], landed.at[me * local + j], own_out).start()

        @pl.loop(1, n)
        def _(k):
            to = lax.rem(me + k, n)
            theirs = pl.ds(pl.multiple_of(to * shots, shots), shots)
            pltpu.make_async_remote_copy(
                prod.at[j, :, theirs, :], landed.at[me * local + j], out_send, out_recv,
                device_id={"shot": to}, device_id_type=MESH).start()

    others = pl.ds(0, (n - 1) * local)
    pltpu.make_async_copy(landed.at[pl.ds(0, local)], landed.at[pl.ds(0, local)], own_out).wait()
    pltpu.make_async_copy(send.at[others], send.at[others], in_send).wait()
    pltpu.make_async_copy(landed.at[others], landed.at[others], out_send).wait()
    pltpu.make_async_copy(landed.at[others], landed.at[others], out_recv).wait()
    out = pltpu.make_async_copy(landed, o_ref, load_sem)
    out.start()
    out.wait()


def shards(n, spectra, fold_counts, inverse_wavelet):
    shots, _, bins, points = spectra.shape
    local = bins // n
    vmem = pl.BlockSpec(memory_space=pltpu.VMEM)
    bf16 = jnp.bfloat16
    landed = pl.pallas_call(
        functools.partial(exchange_kernel, n),
        out_shape=jax.ShapeDtypeStruct((bins, 2, shots, points), bf16),
        in_specs=[vmem, vmem, vmem, pl.BlockSpec(memory_space=pltpu.SMEM)],
        out_specs=pl.BlockSpec(memory_space=pl.ANY),
        scratch_shapes=[
            pltpu.VMEM((points // 128, shots * 2 * bins, 128), jnp.float32),
            pltpu.VMEM((bins, 2, shots, points), bf16),
            pltpu.VMEM((local, 2, points, points), bf16),
            pltpu.VMEM((local, 2, points, points), bf16),
            pltpu.VMEM((bins, 2, shots, points), bf16),
            pltpu.VMEM((points, points), bf16),
            pltpu.VMEM((points, points), bf16),
            pltpu.VMEM((points, points), bf16),
            pltpu.SemaphoreType.DMA,
            pltpu.SemaphoreType.DMA((local,)),
            pltpu.SemaphoreType.DMA,
            pltpu.SemaphoreType.DMA,
            pltpu.SemaphoreType.DMA,
            pltpu.SemaphoreType.DMA,
        ],
        compiler_params=pltpu.CompilerParams(
            collective_id=0, has_side_effects=True, vmem_limit_bytes=VMEM_BYTES),
    )(spectra, fold_counts[:, None], fold_counts[None, :], inverse_wavelet)
    return landed.transpose(2, 1, 0, 3)


def solution(mesh):
    spec = P(("groups", "shot"), None, None, None)
    return jax.shard_map(functools.partial(shards, mesh.shape["shot"]), mesh=mesh,
                         in_specs=(spec, P("groups"), P()), out_specs=spec, check_vma=False)
```

```python
import functools

import jax
import jax.numpy as jnp
from jax import lax
from jax.experimental import pallas as pl
from jax.experimental.pallas import tpu as pltpu
from jax.sharding import PartitionSpec as P

MESH = pl.DeviceIdType.MESH
VMEM_BYTES = 56 * 1024 * 1024


def turn(eye, block):
    return lax.dot_general(eye, block, (((1,), (1,)), ((), ())),
                           preferred_element_type=jnp.float32).astype(jnp.bfloat16)


def exchange_kernel(n, x_hbm, row_ref, wave_ref, o_ref,
                    x_ref, stage, send, recv, prod, keep, swap, eye,
                    load_sem, own_in, in_send, in_recv, out_send, out_recv, own_out):
    shots, _, bins, points = x_ref.shape
    local = bins // n
    me = lax.axis_index("shot")
    mine = pl.ds(pl.multiple_of(me * shots, shots), shots)
    barrier = pltpu.get_barrier_semaphore()
    chunks = load_sem.shape[0]
    chunk = shots // chunks

    def load(i):
        rows = pl.ds(i * chunk, chunk)
        return pltpu.make_async_copy(x_hbm.at[rows], x_ref.at[rows], load_sem.at[i])

    for i in range(chunks):
        load(i).start()

    @pl.loop(1, n)
    def _(k):
        pl.semaphore_signal(barrier, inc=1, device_id={"shot": lax.rem(me + k, n)}, device_id_type=MESH)

    for i in range(chunks):
        load(i).wait()

        @pl.loop(i * chunk, (i + 1) * chunk)
        def _(s):
            rows = x_ref[s].reshape(2 * bins, points).astype(jnp.float32)
            for q in range(points // 128):
                stage[q, pl.ds(pl.multiple_of(s * 2 * bins, 2 * bins), 2 * bins), :] = rows[:, q * 128 : q * 128 + 128]

    def gather(f):
        for c in range(2):
            for q in range(points // 128):
                traces = stage[q, pl.ds(c * bins + f, shots, stride=2 * bins), :]
                send[f, c, :, pl.ds(q * 128, 128)] = traces.astype(jnp.bfloat16)

    pl.semaphore_wait(barrier, n - 1)

    @pl.loop(0, local)
    def _(j):
        @pl.loop(1, n)
        def _(k):
            to = lax.rem(me + k, n)
            gather(to * local + j)
            pltpu.make_async_remote_copy(
                send.at[to * local + j], recv.at[j, :, mine, :], in_send, in_recv.at[j],
                device_id={"shot": to}, device_id_type=MESH).start()

        gather(me * local + j)
        pltpu.make_async_copy(send.at[me * local + j], recv.at[j, :, mine, :], own_in.at[j]).start()

    shot = lax.broadcasted_iota(jnp.int32, (points, points), 0)
    point = lax.broadcasted_iota(jnp.int32, (points, points), 1)
    eye[...] = jnp.where(shot == point, 1.0, 0.0).astype(jnp.bfloat16)
    mirrored = jnp.where(jnp.abs(shot - point) < row_ref[...], 1.0, 0.0).astype(jnp.bfloat16)
    keep[...] = turn(eye[...], mirrored)
    swap[...] = keep[...] * (1.0 - mirrored)

    @pl.loop(0, local)
    def _(j):
        pltpu.make_async_copy(send.at[me * local + j], recv.at[j, :, mine, :], own_in.at[j]).wait()
        rest = pl.ds(0, (n - 1) * shots)
        pltpu.make_async_copy(recv.at[j, :, rest, :], recv.at[j, :, rest, :], in_recv.at[j]).wait()
        for c in range(2):
            block = recv[j, c]
            recv[j, c] = block * keep[...] + turn(eye[...], block * swap[...])
        wave_real = wave_ref[0, me * local + j]
        wave_imag = wave_ref[1, me * local + j]
        tile = min(points, 256)

        @pl.loop(0, points // tile)
        def _(t):
            part = pl.ds(pl.multiple_of(t * tile, tile), tile)
            left_real, left_imag = recv[j, 0, part, :], recv[j, 1, part, :]
            real, imag = recv[j, 0], recv[j, 1]
            dot = functools.partial(jnp.dot, preferred_element_type=jnp.float32)
            prod_real = dot(left_real, real) - dot(left_imag, imag)
            prod_imag = dot(left_real, imag) + dot(left_imag, real)
            prod[j, 0, part, :] = (-(wave_real * prod_real - wave_imag * prod_imag)).astype(jnp.bfloat16)
            prod[j, 1, part, :] = (-(wave_real * prod_imag + wave_imag * prod_real)).astype(jnp.bfloat16)

        pltpu.make_async_copy(prod.at[j, :, mine, :], o_ref.at[me * local + j], own_out).start()

        @pl.loop(1, n)
        def _(k):
            to = lax.rem(me + k, n)
            theirs = pl.ds(pl.multiple_of(to * shots, shots), shots)
            pltpu.make_async_remote_copy(
                prod.at[j, :, theirs, :], o_ref.at[me * local + j], out_send, out_recv,
                device_id={"shot": to}, device_id_type=MESH).start()

    others = pl.ds(0, (n - 1) * local)
    pltpu.make_async_copy(o_ref.at[pl.ds(0, local)], o_ref.at[pl.ds(0, local)], own_out).wait()
    pltpu.make_async_copy(send.at[others], send.at[others], in_send).wait()
    pltpu.make_async_copy(o_ref.at[others], o_ref.at[others], out_send).wait()
    pltpu.make_async_copy(o_ref.at[others], o_ref.at[others], out_recv).wait()

def regroup_kernel(x_ref, o_ref, stage):
    bins, _, shots, points = x_ref.shape

    @pl.loop(0, bins)
    def _(f):
        rows = x_ref[f, 0].astype(jnp.float32)
        for q in range(points // 128):
            stage[q, pl.ds(pl.multiple_of(f * shots, shots), shots), :] = rows[:, q * 128 : q * 128 + 128]

    @pl.loop(0, shots)
    def _(s):
        for q in range(points // 128):
            o_ref[s, 0, :, pl.ds(q * 128, 128)] = stage[q, pl.ds(s, bins, stride=shots), :].astype(jnp.bfloat16)


def shards(n, spectra, fold_counts, inverse_wavelet):
    shots, _, bins, points = spectra.shape
    local = bins // n
    bf16 = jnp.bfloat16
    landed = pl.pallas_call(
        functools.partial(exchange_kernel, n),
        out_shape=jax.ShapeDtypeStruct((bins, 2, shots, points), bf16),
        in_specs=[pl.BlockSpec(memory_space=pl.ANY), pl.BlockSpec(memory_space=pltpu.VMEM),
                  pl.BlockSpec(memory_space=pltpu.SMEM)],
        out_specs=pl.BlockSpec(memory_space=pl.ANY),
        scratch_shapes=[
            pltpu.VMEM(spectra.shape, bf16),
            pltpu.VMEM((points // 128, shots * 2 * bins, 128), jnp.float32),
            pltpu.VMEM((bins, 2, shots, points), bf16),
            pltpu.VMEM((local, 2, points, points), bf16),
            pltpu.VMEM((local, 2, points, points), bf16),
            pltpu.VMEM((points, points), bf16),
            pltpu.VMEM((points, points), bf16),
            pltpu.VMEM((points, points), bf16),
            pltpu.SemaphoreType.DMA((4,)),
            pltpu.SemaphoreType.DMA((local,)),
            pltpu.SemaphoreType.DMA,
            pltpu.SemaphoreType.DMA((local,)),
            pltpu.SemaphoreType.DMA,
            pltpu.SemaphoreType.DMA,
            pltpu.SemaphoreType.DMA,
        ],
        compiler_params=pltpu.CompilerParams(
            collective_id=0, has_side_effects=True, vmem_limit_bytes=VMEM_BYTES),
    )(spectra, fold_counts[None, :], inverse_wavelet)
    few = min(shots, 16)
    return pl.pallas_call(
        regroup_kernel,
        grid=(shots // few, 2),
        out_shape=jax.ShapeDtypeStruct(spectra.shape, bf16),
        in_specs=[pl.BlockSpec((bins, 1, few, points), lambda s, c: (0, c, s, 0))],
        out_specs=pl.BlockSpec((few, 1, bins, points), lambda s, c: (s, c, 0, 0)),
        scratch_shapes=[pltpu.VMEM((points // 128, bins * few, 128), jnp.float32)],
    )(landed)


def solution(mesh):
    spec = P(("groups", "shot"), None, None, None)
    return jax.shard_map(functools.partial(shards, mesh.shape["shot"]), mesh=mesh,
                         in_specs=(spec, P("groups"), P()), out_specs=spec, check_vma=False)
```

```python
import functools

import jax
import jax.numpy as jnp
from jax import lax
from jax.experimental import pallas as pl
from jax.experimental.pallas import tpu as pltpu
from jax.sharding import PartitionSpec as P

MESH = pl.DeviceIdType.MESH
VMEM_BYTES = 56 * 1024 * 1024


def turn(eye, block):
    return lax.dot_general(eye, block, (((1,), (1,)), ((), ())),
                           preferred_element_type=jnp.float32).astype(jnp.bfloat16)


def exchange_kernel(n, x_hbm, row_ref, wave_ref, o_ref,
                    x_ref, stage, send, recv, prod, keep, swap, eye,
                    load_sem, own_in, in_send, in_recv, out_send, out_recv, own_out):
    shots, _, bins, points = x_ref.shape
    local = bins // n
    me = lax.axis_index("shot")
    mine = pl.ds(pl.multiple_of(me * shots, shots), shots)
    barrier = pltpu.get_barrier_semaphore()
    chunks = load_sem.shape[0]
    chunk = shots // chunks

    def load(i):
        rows = pl.ds(i * chunk, chunk)
        return pltpu.make_async_copy(x_hbm.at[rows], x_ref.at[rows], load_sem.at[i])

    for i in range(chunks):
        load(i).start()

    @pl.loop(1, n)
    def _(k):
        pl.semaphore_signal(barrier, inc=1, device_id={"shot": lax.rem(me + k, n)}, device_id_type=MESH)

    for i in range(chunks):
        load(i).wait()

        @pl.loop(i * chunk, (i + 1) * chunk)
        def _(s):
            rows = x_ref[s].reshape(2 * bins, points).astype(jnp.float32)
            for q in range(points // 128):
                stage[q, pl.ds(pl.multiple_of(s * 2 * bins, 2 * bins), 2 * bins), :] = rows[:, q * 128 : q * 128 + 128]

    def gather(f):
        for c in range(2):
            for q in range(points // 128):
                traces = stage[q, pl.ds(c * bins + f, shots, stride=2 * bins), :]
                send[f, c, :, pl.ds(q * 128, 128)] = traces.astype(jnp.bfloat16)

    pl.semaphore_wait(barrier, n - 1)

    @pl.loop(0, local)
    def _(j):
        @pl.loop(1, n)
        def _(k):
            to = lax.rem(me + k, n)
            gather(to * local + j)
            pltpu.make_async_remote_copy(
                send.at[to * local + j], recv.at[j, :, mine, :], in_send, in_recv.at[j],
                device_id={"shot": to}, device_id_type=MESH).start()

        gather(me * local + j)
        pltpu.make_async_copy(send.at[me * local + j], recv.at[j, :, mine, :], own_in.at[j]).start()

    shot = lax.broadcasted_iota(jnp.int32, (points, points), 0)
    point = lax.broadcasted_iota(jnp.int32, (points, points), 1)
    eye[...] = jnp.where(shot == point, 1.0, 0.0).astype(jnp.bfloat16)
    mirrored = jnp.where(jnp.abs(shot - point) < row_ref[...], 1.0, 0.0).astype(jnp.bfloat16)
    keep[...] = turn(eye[...], mirrored)
    swap[...] = keep[...] * (1.0 - mirrored)

    @pl.loop(0, local)
    def _(j):
        pltpu.make_async_copy(send.at[me * local + j], recv.at[j, :, mine, :], own_in.at[j]).wait()
        rest = pl.ds(0, (n - 1) * shots)
        pltpu.make_async_copy(recv.at[j, :, rest, :], recv.at[j, :, rest, :], in_recv.at[j]).wait()
        for c in range(2):
            block = recv[j, c]
            recv[j, c] = block * keep[...] + turn(eye[...], block * swap[...])
        wave_real = wave_ref[0, me * local + j]
        wave_imag = wave_ref[1, me * local + j]
        tile = min(points, 256)

        @pl.loop(0, points // tile)
        def _(t):
            part = pl.ds(pl.multiple_of(t * tile, tile), tile)
            left_real, left_imag = recv[j, 0, part, :], recv[j, 1, part, :]
            real, imag = recv[j, 0], recv[j, 1]
            dot = functools.partial(jnp.dot, preferred_element_type=jnp.float32)
            prod_real = dot(left_real, real) - dot(left_imag, imag)
            prod_imag = dot(left_real, imag) + dot(left_imag, real)
            prod[j, 0, part, :] = (-(wave_real * prod_real - wave_imag * prod_imag)).astype(jnp.bfloat16)
            prod[j, 1, part, :] = (-(wave_real * prod_imag + wave_imag * prod_real)).astype(jnp.bfloat16)

        pltpu.make_async_copy(prod.at[j, :, mine, :], o_ref.at[me * local + j], own_out).start()

        @pl.loop(1, n)
        def _(k):
            to = lax.rem(me + k, n)
            theirs = pl.ds(pl.multiple_of(to * shots, shots), shots)
            pltpu.make_async_remote_copy(
                prod.at[j, :, theirs, :], o_ref.at[me * local + j], out_send, out_recv,
                device_id={"shot": to}, device_id_type=MESH).start()

    others = pl.ds(0, (n - 1) * local)
    pltpu.make_async_copy(o_ref.at[pl.ds(0, local)], o_ref.at[pl.ds(0, local)], own_out).wait()
    pltpu.make_async_copy(send.at[others], send.at[others], in_send).wait()
    pltpu.make_async_copy(o_ref.at[others], o_ref.at[others], out_send).wait()
    pltpu.make_async_copy(o_ref.at[others], o_ref.at[others], out_recv).wait()

def regroup_kernel(x_ref, o_ref):
    for q in range(x_ref.shape[3] // 128):
        lanes = pl.ds(q * 128, 128)
        o_ref[:, 0, :, lanes] = jnp.swapaxes(x_ref[:, 0, :, lanes], 0, 1)


def shards(n, spectra, fold_counts, inverse_wavelet):
    shots, _, bins, points = spectra.shape
    local = bins // n
    bf16 = jnp.bfloat16
    landed = pl.pallas_call(
        functools.partial(exchange_kernel, n),
        out_shape=jax.ShapeDtypeStruct((bins, 2, shots, points), bf16),
        in_specs=[pl.BlockSpec(memory_space=pl.ANY), pl.BlockSpec(memory_space=pltpu.VMEM),
                  pl.BlockSpec(memory_space=pltpu.SMEM)],
        out_specs=pl.BlockSpec(memory_space=pl.ANY),
        scratch_shapes=[
            pltpu.VMEM(spectra.shape, bf16),
            pltpu.VMEM((points // 128, shots * 2 * bins, 128), jnp.float32),
            pltpu.VMEM((bins, 2, shots, points), bf16),
            pltpu.VMEM((local, 2, points, points), bf16),
            pltpu.VMEM((local, 2, points, points), bf16),
            pltpu.VMEM((points, points), bf16),
            pltpu.VMEM((points, points), bf16),
            pltpu.VMEM((points, points), bf16),
            pltpu.SemaphoreType.DMA((4,)),
            pltpu.SemaphoreType.DMA((local,)),
            pltpu.SemaphoreType.DMA,
            pltpu.SemaphoreType.DMA((local,)),
            pltpu.SemaphoreType.DMA,
            pltpu.SemaphoreType.DMA,
            pltpu.SemaphoreType.DMA,
        ],
        compiler_params=pltpu.CompilerParams(
            collective_id=0, has_side_effects=True, vmem_limit_bytes=VMEM_BYTES),
    )(spectra, fold_counts[None, :], inverse_wavelet)
    few = min(shots, 16)
    return pl.pallas_call(
        regroup_kernel,
        grid=(shots // few, 2),
        out_shape=jax.ShapeDtypeStruct(spectra.shape, bf16),
        in_specs=[pl.BlockSpec((bins, 1, few, points), lambda s, c: (0, c, s, 0))],
        out_specs=pl.BlockSpec((few, 1, bins, points), lambda s, c: (s, c, 0, 0)),
    )(landed)


def solution(mesh):
    spec = P(("groups", "shot"), None, None, None)
    return jax.shard_map(functools.partial(shards, mesh.shape["shot"]), mesh=mesh,
                         in_specs=(spec, P("groups"), P()), out_specs=spec, check_vma=False)
```
